128 devices in a mesh: gx: 8 (over y, z_hi), gy: 16 (over x, z_lo, core).
Axes of the slice: x: 4, y: 4, z: 4 (z_hi: 2, z_lo: 2; z = z_hi * 2 + z_lo), core: 2. Of those that a mesh axis runs over, the one named last changes fastest.
Arguments:
- images: float32 [128, 256, 32, 32], P(('gx', 'gy')), may hold values from -6 to 6
- blocks: float32 [2, 1024, 512, 512], P(None, ('gx', 'gy')), may hold values from -0.25 to 0.25
- bias: float32 [2, 256], replicated, may hold values from -3 to 3
Outputs:
- features: float32 [128, 256, 32, 32], P(('gx', 'gy'))
The draws below stay inside these ranges and needn't reach their ends.
All inputs are finite; a program needn't handle non-finite values.
Results may differ from the reference program's by a relative error of at most 0.0001.
Values sent between devices are 32-bit elements; how exact they have to be, the bound alone decides.
No kernel may reach another device: no remote copies, remote signals or barrier semaphores. Data moves between devices by JAX's collectives and lax.ppermute only.
A program may use at most 128 MiB of HBM per device.

```python
import jax
import jax.numpy as jnp
from jax import lax

C = 256
H = 32
W = 32
LAYERS = 2
CH2 = 512
FREQ = 1024
IMAGES = 128


def levels(key, shape, pieces, smallest, high):
    gain, own = 1.0, jax.random.fold_in(key, 6)
    for axis_at, blocks in pieces:
        draws = jnp.exp(jax.random.uniform(jax.random.fold_in(own, axis_at), (blocks,), jnp.float32, smallest / len(pieces), high / len(pieces)))
        gain = gain * jnp.repeat(draws, shape[axis_at] // blocks).reshape([-1 if axis == axis_at else 1 for axis in range(len(shape))])
    return gain


def normal_values(stream_key, shape, scale, reach, split=(), kind=jnp.bfloat16):
    values = scale * jax.random.normal(stream_key, shape, jnp.float32)
    if split:
        values = values * levels(stream_key, shape, split, -0.22, 0.18)
    return jnp.clip(values, -reach, reach).astype(kind)


def setup_inputs(seed: int = 0) -> dict:
    key_list = jax.random.split(jax.random.key(seed), 4)
    images = normal_values(key_list[0], (IMAGES, C, H, W), 1.0, 6.0, ((0, 128),), jnp.float32)
    blocks = normal_values(key_list[1], (LAYERS, FREQ, CH2, CH2), (2 * C) ** -0.5, 0.25, ((1, 128),), jnp.float32)
    bias = normal_values(key_list[2], (LAYERS, C), 0.5, 3.0, (), jnp.float32)
    return dict(images=images, blocks=blocks, bias=bias)


def reference(images, blocks, bias):
    activity = images
    for layer_index in range(LAYERS):
        spectrum = jnp.fft.fft2(activity, axes=(2, 3), norm="ortho")
        vectors = jnp.concatenate([jnp.real(spectrum), jnp.imag(spectrum)], axis=1)
        vectors = vectors.reshape(IMAGES, 2 * C, H * W).transpose(2, 0, 1)
        mixture = jnp.einsum("fnk,fjk->fnj", vectors, blocks[layer_index], precision=lax.Precision.HIGHEST)
        mixture = mixture.transpose(1, 2, 0).reshape(IMAGES, 2 * C, H, W)
        complex_spec = lax.complex(mixture[:, :C], mixture[:, C:])
        response = jnp.real(jnp.fft.ifft2(complex_spec, axes=(2, 3), norm="ortho"))
        activity = jax.nn.relu(response + bias[layer_index][None, :, None, None])
    return activity
```

```python
import functools
import math

import jax
import jax.numpy as jnp
import ml_dtypes
import numpy as np
from jax import lax
from jax.experimental import pallas as pl
from jax.experimental.pallas import tpu as pltpu
from jax.sharding import PartitionSpec as P

BF16 = jnp.bfloat16
F32 = jnp.float32
STEPS = 4
LANES = 128
ROWS = 8


def dot(a, b):
    return jnp.dot(a, b, preferred_element_type=F32)


def dot_nt(a, b):
    return lax.dot_general(a, b, (((1,), (1,)), ((), ())), preferred_element_type=F32)


def split(x):
    hi = x.astype(BF16)
    lo = (x - hi.astype(F32)).astype(BF16)
    return hi, lo


def split_table(table):
    hi = table.astype(ml_dtypes.bfloat16)
    lo = (table - hi.astype(np.float64)).astype(ml_dtypes.bfloat16)
    return hi, lo


def transform_tables(height, width):
    half = height // 2
    pixels = height * width
    h = np.arange(half)[:, None]
    w = np.arange(width)[None, :]
    v = np.arange(width)[:, None, None]
    forward, inverse = [], []
    for parity in range(2):
        u = 2 * np.arange(half)[:, None, None, None] + parity
        angle = 2.0 * math.pi * ((u * h) / height + (v * w) / width)
        scale = 1.0 / math.sqrt(pixels)
        table = np.stack([np.cos(angle) * scale, -np.sin(angle) * scale], axis=1)
        table = table.reshape(half, 2, width, half * width)
        forward.append(split_table(table))
        back = np.transpose(table, (3, 1, 0, 2)).reshape(half * width, pixels)
        inverse.append(split_table(back))
    return forward, inverse


def fold(x, xs):
    rows = x.shape[0] // 2
    top, bottom = x[:rows], x[rows:]
    for parity, value in enumerate((top + bottom, top - bottom)):
        xs[parity, 0], xs[parity, 1] = split(value)


def forward_part(tables, xs, out_ref):
    for parity in range(2):
        hi_ref, lo_ref = tables[2 * parity], tables[2 * parity + 1]
        units, _, width, depth = hi_ref.shape
        f_hi = hi_ref[...].reshape(units * 2 * width, depth)
        f_lo = lo_ref[...].reshape(units * 2 * width, depth)
        part = dot(f_hi, xs[parity, 0]) + dot(f_hi, xs[parity, 1]) + dot(f_lo, xs[parity, 0])
        groups = part.shape[-1] // LANES
        part = part.reshape(units, 2, width // ROWS, ROWS, groups * LANES)
        for piece in range(2):
            for group in range(groups):
                lanes = slice(group * LANES, (group + 1) * LANES)
                out_ref[:, parity, :, piece * groups + group] = part[:, piece, :, :, lanes]


def forward_kernel(x_ref, e_hi, e_lo, o_hi, o_lo, out_ref, xs):
    @pl.when(pl.program_id(0) == 0)
    def _():
        fold(x_ref[...], xs)

    forward_part((e_hi, e_lo, o_hi, o_lo), xs, out_ref)


def forward(x, tables):
    pixels, channels = x.shape
    half, _, width, depth = tables[0].shape
    units = half // STEPS
    shape = (2, width // ROWS, 2 * channels // LANES, ROWS, LANES)
    table_spec = pl.BlockSpec((units, 2, width, depth), lambda s: (s, 0, 0, 0))
    out = pl.pallas_call(
        forward_kernel,
        grid=(STEPS,),
        in_specs=[pl.BlockSpec((pixels, channels), lambda s: (0, 0))] + [table_spec] * 4,
        out_specs=pl.BlockSpec((units,) + shape, lambda s: (s, 0, 0, 0, 0, 0)),
        out_shape=jax.ShapeDtypeStruct((half,) + shape, F32),
        scratch_shapes=[pltpu.VMEM((2, 2, pixels // 2, channels), BF16)],
        compiler_params=pltpu.CompilerParams(vmem_limit_bytes=24 << 20),
        name="forward_transform",
    )(x, *tables)
    return out


def inverse_value(m_ref, tables, bias_ref):
    half, _, blocks, groups, _, _ = m_ref.shape
    rows = half * blocks * ROWS
    parts = []
    for parity in range(2):
        m = [m_ref[:, parity, :, group].reshape(rows, LANES) for group in range(groups)]
        real = jnp.concatenate(m[: groups // 2], axis=1)
        imag = jnp.concatenate(m[groups // 2 :], axis=1)
        m = jnp.concatenate([real, imag], axis=0)
        m_hi, m_lo = split(m)
        g_hi, g_lo = tables[2 * parity][...], tables[2 * parity + 1][...]
        parts.append(dot(g_hi, m_hi) + dot(g_hi, m_lo) + dot(g_lo, m_hi))
    even, odd = parts
    bias = bias_ref[...]
    return jnp.maximum(even + odd + bias, 0.0), jnp.maximum(even - odd + bias, 0.0)


def inverse_kernel(m_ref, e_hi, e_lo, o_hi, o_lo, bias_ref, out_ref):
    top, bottom = inverse_value(m_ref, (e_hi, e_lo, o_hi, o_lo), bias_ref)
    rows = top.shape[0]
    out_ref[:rows] = top
    out_ref[rows:] = bottom


def inverse(m, tables, bias):
    pixels = 2 * tables[0].shape[0]
    channels = bias.shape[1]
    return pl.pallas_call(
        inverse_kernel,
        out_shape=jax.ShapeDtypeStruct((pixels, channels), F32),
        compiler_params=pltpu.CompilerParams(vmem_limit_bytes=24 << 20),
        name="inverse_transform",
    )(m, *tables, bias)


def turn_kernel(m_ref, ge_hi, ge_lo, go_hi, go_lo, bias_ref, e_hi, e_lo, o_hi, o_lo, out_ref, xs):
    top, bottom = inverse_value(m_ref, (ge_hi, ge_lo, go_hi, go_lo), bias_ref)
    for parity, value in enumerate((top + bottom, top - bottom)):
        xs[parity, 0], xs[parity, 1] = split(value)
    forward_part((e_hi, e_lo, o_hi, o_lo), xs, out_ref)


def turn(m, back_tables, bias, tables):
    channels = bias.shape[1]
    return pl.pallas_call(
        turn_kernel,
        out_shape=jax.ShapeDtypeStruct(m.shape, F32),
        scratch_shapes=[pltpu.VMEM((2, 2, back_tables[0].shape[0], channels), BF16)],
        compiler_params=pltpu.CompilerParams(vmem_limit_bytes=32 << 20),
        name="turn",
    )(m, *back_tables, bias, *tables)


def mix_kernel(per, v_ref, a_ref, out_ref):
    i = pl.program_id(0)
    both = a_ref.shape[-1]
    groups = both // LANES
    stride = groups * per
    images = v_ref.shape[0] // stride
    rows = [pl.ds(group * per + i, images, stride=stride) for group in range(groups)]
    v_hi, v_lo = split(jnp.concatenate([v_ref[r, :] for r in rows], axis=1))
    a_hi, a_lo = split(a_ref[0])
    out = dot_nt(v_hi, a_hi) + dot_nt(v_hi, a_lo) + dot_nt(v_lo, a_hi)
    for group, r in enumerate(rows):
        out_ref[r, :] = out[:, group * LANES : (group + 1) * LANES]


def mix(v, blocks, layer):
    _, per, both, _ = blocks.shape
    return pl.pallas_call(
        functools.partial(mix_kernel, per),
        grid=(per,),
        in_specs=[
            pl.BlockSpec(v.shape, lambda i: (0, 0)),
            pl.BlockSpec((None, 1, both, both), lambda i: (layer, i, 0, 0)),
        ],
        out_specs=pl.BlockSpec(v.shape, lambda i: (0, 0)),
        out_shape=jax.ShapeDtypeStruct(v.shape, F32),
        compiler_params=pltpu.CompilerParams(vmem_limit_bytes=24 << 20),
        name="mix",
    )(v, blocks)


def body(images, blocks, bias):
    _, channels, height, width = images.shape
    pixels = height * width
    forward_np, inverse_np = transform_tables(height, width)
    tables = [jnp.asarray(t) for pair in forward_np for t in pair]
    back_tables = [jnp.asarray(t) for pair in inverse_np for t in pair]

    def exchange(value):
        return lax.all_to_all(value, ("gx", "gy"), split_axis=0, concat_axis=0, tiled=True)

    parts = lax.axis_size(("gx", "gy"))
    sent = (parts, 2 * channels // LANES, ROWS, LANES)
    flat = (-1, LANES)

    def mixed(v, layer):
        held = exchange(v.reshape(sent)).reshape(flat)
        return exchange(mix(held, blocks, layer).reshape(sent)).reshape(v.shape)

    x = images.reshape(channels, pixels).T
    m = mixed(forward(x, tables), 0)
    m = mixed(turn(m, back_tables, bias[0:1], tables), 1)
    out = inverse(m, back_tables, bias[1:2])
    return out.T.reshape(1, channels, height, width)


def solution(mesh):
    placed = (P(("gx", "gy"), None, None, None), P(None, ("gx", "gy"), None, None), P())
    return jax.shard_map(
        body,
        mesh=mesh,
        in_specs=placed,
        out_specs=P(("gx", "gy"), None, None, None),
        check_vma=False,
    )
```

```python
import functools
import math

import jax
import jax.numpy as jnp
import ml_dtypes
import numpy as np
from jax import lax
from jax.experimental import pallas as pl
from jax.experimental.pallas import tpu as pltpu
from jax.sharding import PartitionSpec as P

BF16 = jnp.bfloat16
F32 = jnp.float32
STEPS = 4
LANES = 128
ROWS = 8


def cost(products, arrays):
    bytes_accessed = sum(math.prod(a.shape) * a.dtype.itemsize for a in arrays)
    return pl.CostEstimate(flops=6 * products, bytes_accessed=bytes_accessed, transcendentals=0)


def dot(a, b):
    return jnp.dot(a, b, preferred_element_type=F32)


def dot_nt(a, b):
    return lax.dot_general(a, b, (((1,), (1,)), ((), ())), preferred_element_type=F32)


def split(x):
    hi = x.astype(BF16)
    lo = (x - hi.astype(F32)).astype(BF16)
    return hi, lo


def split_table(table):
    hi = table.astype(ml_dtypes.bfloat16)
    lo = (table - hi.astype(np.float64)).astype(ml_dtypes.bfloat16)
    return hi, lo


def transform_tables(height, width):
    half = height // 2
    pixels = height * width
    h = np.arange(half)[:, None]
    w = np.arange(width)[None, :]
    v = np.arange(width)[:, None, None]
    forward, inverse = [], []
    for parity in range(2):
        u = 2 * np.arange(half)[:, None, None, None] + parity
        angle = 2.0 * math.pi * ((u * h) / height + (v * w) / width)
        scale = 1.0 / math.sqrt(pixels)
        table = np.stack([np.cos(angle) * scale, -np.sin(angle) * scale], axis=1)
        table = table.reshape(half, 2, width, half * width)
        forward.append(split_table(table))
        back = np.transpose(table, (3, 1, 0, 2)).reshape(half * width, pixels)
        inverse.append(split_table(back))
    return forward, inverse


def fold(x, xs):
    rows = x.shape[0] // 2
    top, bottom = x[:rows], x[rows:]
    for parity, value in enumerate((top + bottom, top - bottom)):
        xs[parity, 0], xs[parity, 1] = split(value)


def forward_part(tables, xs, out_ref):
    for parity in range(2):
        hi_ref, lo_ref = tables[2 * parity], tables[2 * parity + 1]
        units, _, width, depth = hi_ref.shape
        f_hi = hi_ref[...].reshape(units * 2 * width, depth)
        f_lo = lo_ref[...].reshape(units * 2 * width, depth)
        part = dot(f_hi, xs[parity, 0]) + dot(f_hi, xs[parity, 1]) + dot(f_lo, xs[parity, 0])
        groups = part.shape[-1] // LANES
        part = part.reshape(units, 2, width // ROWS, ROWS, groups * LANES)
        for piece in range(2):
            for group in range(groups):
                lanes = slice(group * LANES, (group + 1) * LANES)
                out_ref[:, parity, :, piece * groups + group] = part[:, piece, :, :, lanes]


def forward_kernel(x_ref, e_hi, e_lo, o_hi, o_lo, out_ref, xs):
    @pl.when(pl.program_id(0) == 0)
    def _():
        fold(x_ref[...], xs)

    forward_part((e_hi, e_lo, o_hi, o_lo), xs, out_ref)


def forward(x, tables):
    pixels, channels = x.shape
    half, _, width, depth = tables[0].shape
    units = half // STEPS
    shape = (2, width // ROWS, 2 * channels // LANES, ROWS, LANES)
    table_spec = pl.BlockSpec((units, 2, width, depth), lambda s: (s, 0, 0, 0))
    out = pl.pallas_call(
        forward_kernel,
        grid=(STEPS,),
        in_specs=[pl.BlockSpec((pixels, channels), lambda s: (0, 0))] + [table_spec] * 4,
        out_specs=pl.BlockSpec((units,) + shape, lambda s: (s, 0, 0, 0, 0, 0)),
        out_shape=jax.ShapeDtypeStruct((half,) + shape, F32),
        scratch_shapes=[pltpu.VMEM((2, 2, pixels // 2, channels), BF16)],
        compiler_params=pltpu.CompilerParams(vmem_limit_bytes=16 << 20),
        cost_estimate=cost(3 * pixels * pixels * channels, (x, *tables, x, x)),
        name="forward_transform",
    )(*(pltpu.with_memory_space_constraint(a, pltpu.HBM) for a in (x, *tables)))
    return out


def inverse_value(m_ref, tables, bias_ref, layer):
    half, _, blocks, groups, _, _ = m_ref.shape
    rows = half * blocks * ROWS
    parts = []
    for parity in range(2):
        m = [m_ref[:, parity, :, group].reshape(rows, LANES) for group in range(groups)]
        real = jnp.concatenate(m[: groups // 2], axis=1)
        imag = jnp.concatenate(m[groups // 2 :], axis=1)
        m = jnp.concatenate([real, imag], axis=0)
        m_hi, m_lo = split(m)
        g_hi, g_lo = tables[2 * parity][...], tables[2 * parity + 1][...]
        parts.append(dot(g_hi, m_hi) + dot(g_hi, m_lo) + dot(g_lo, m_hi))
    even, odd = parts
    bias = bias_ref[layer : layer + 1, :]
    return jnp.maximum(even + odd + bias, 0.0), jnp.maximum(even - odd + bias, 0.0)


def inverse_kernel(layer, m_ref, e_hi, e_lo, o_hi, o_lo, bias_ref, out_ref):
    top, bottom = inverse_value(m_ref, (e_hi, e_lo, o_hi, o_lo), bias_ref, layer)
    rows = top.shape[0]
    out_ref[:rows] = top
    out_ref[rows:] = bottom


def inverse(m, tables, bias, layer):
    pixels = 2 * tables[0].shape[0]
    channels = bias.shape[1]
    return pl.pallas_call(
        functools.partial(inverse_kernel, layer),
        out_shape=jax.ShapeDtypeStruct((pixels, channels), F32),
        compiler_params=pltpu.CompilerParams(vmem_limit_bytes=16 << 20),
        cost_estimate=cost(pixels * pixels * channels, (m, *tables, m)),
        name="inverse_transform",
    )(m, *tables, bias)


def turn_kernel(layer, m_ref, ge_hi, ge_lo, go_hi, go_lo, bias_ref, e_hi, e_lo, o_hi, o_lo, out_ref, xs):
    top, bottom = inverse_value(m_ref, (ge_hi, ge_lo, go_hi, go_lo), bias_ref, layer)
    for parity, value in enumerate((top + bottom, top - bottom)):
        xs[parity, 0], xs[parity, 1] = split(value)
    forward_part((e_hi, e_lo, o_hi, o_lo), xs, out_ref)


def turn(m, back_tables, bias, layer, tables):
    channels = bias.shape[1]
    return pl.pallas_call(
        functools.partial(turn_kernel, layer),
        out_shape=jax.ShapeDtypeStruct(m.shape, F32),
        scratch_shapes=[pltpu.VMEM((2, 2, back_tables[0].shape[0], channels), BF16)],
        compiler_params=pltpu.CompilerParams(vmem_limit_bytes=16 << 20),
        cost_estimate=cost(8 * tables[0].size * channels, (m, *back_tables, *tables, m)),
        name="turn",
    )(m, *back_tables, bias, *tables)


def mix_kernel(layer, v_ref, a_ref, out_ref):
    _, per, both, _ = a_ref.shape
    groups = both // LANES
    stride = groups * per
    images = v_ref.shape[0] // stride
    for i in range(per):
        rows = [pl.ds(group * per + i, images, stride=stride) for group in range(groups)]
        v_hi, v_lo = split(jnp.concatenate([v_ref[r, :] for r in rows], axis=1))
        a_hi, a_lo = split(a_ref[layer, i])
        out = dot_nt(v_hi, a_hi) + dot_nt(v_hi, a_lo) + dot_nt(v_lo, a_hi)
        for group, r in enumerate(rows):
            out_ref[r, :] = out[:, group * LANES : (group + 1) * LANES]


def mix(v, blocks, layer):
    return pl.pallas_call(
        functools.partial(mix_kernel, layer),
        in_specs=[pl.BlockSpec(memory_space=pltpu.VMEM)] * 2,
        out_specs=pl.BlockSpec(memory_space=pltpu.VMEM),
        out_shape=jax.ShapeDtypeStruct(v.shape, F32),
        compiler_params=pltpu.CompilerParams(vmem_limit_bytes=12 << 20),
        cost_estimate=cost(v.size * blocks.shape[-1], (v, v, blocks)),
        name="mix",
    )(v, blocks)


def body(images, blocks, bias):
    _, channels, height, width = images.shape
    pixels = height * width
    forward_np, inverse_np = transform_tables(height, width)
    tables = [jnp.asarray(t) for pair in forward_np for t in pair]
    back_tables = [jnp.asarray(t) for pair in inverse_np for t in pair]

    def exchange(value):
        return lax.all_to_all(value, ("gx", "gy"), split_axis=0, concat_axis=0, tiled=True)

    parts = lax.axis_size(("gx", "gy"))
    sent = (parts, 2 * channels // LANES, ROWS, LANES)
    flat = (-1, LANES)

    def returned(value):
        return exchange(value.reshape(sent)).reshape(tables[0].shape[0], 2, -1, 2 * channels // LANES, ROWS, LANES)

    x = images.reshape(channels, pixels).T
    v = forward(x, tables)
    held = exchange(v.reshape(sent))
    m = returned(mix(held.reshape(flat), blocks, 0))
    v = turn(m, back_tables, bias, 0, tables)
    held = exchange(v.reshape(sent))
    m = returned(mix(held.reshape(flat), blocks, 1))
    out = inverse(m, back_tables, bias, 1)
    return out.T.reshape(1, channels, height, width)


def solution(mesh):
    placed = (P(("gx", "gy"), None, None, None), P(None, ("gx", "gy"), None, None), P())
    return jax.shard_map(
        body,
        mesh=mesh,
        in_specs=placed,
        out_specs=P(("gx", "gy"), None, None, None),
        check_vma=False,
    )
```

```python
import functools
import math

import jax
import jax.numpy as jnp
import ml_dtypes
import numpy as np
from jax import lax
from jax.experimental import pallas as pl
from jax.experimental.pallas import tpu as pltpu
from jax.sharding import PartitionSpec as P

BF16 = jnp.bfloat16
F32 = jnp.float32
LANES = 128
ROWS = 8
VMEM = pl.BlockSpec(memory_space=pltpu.VMEM)
HBM = pl.BlockSpec(memory_space=pl.ANY)


def cost(products, arrays):
    bytes_accessed = sum(math.prod(a.shape) * a.dtype.itemsize for a in arrays)
    return pl.CostEstimate(flops=6 * products, bytes_accessed=bytes_accessed, transcendentals=0)


def dot(a, b):
    return jnp.dot(a, b, preferred_element_type=F32)


def dot_nt(a, b):
    return lax.dot_general(a, b, (((1,), (1,)), ((), ())), preferred_element_type=F32)


def split(x):
    hi = x.astype(BF16)
    lo = (x - hi.astype(F32)).astype(BF16)
    return hi, lo


def dot_split(left_both, left_hi, right_hi, right_lo):
    both = dot(left_both, right_hi)
    rows = left_hi.shape[0]
    return both[:rows] + both[rows:] + dot(left_hi, right_lo)


def split_table(table):
    hi = table.astype(ml_dtypes.bfloat16)
    lo = (table - hi.astype(np.float64)).astype(ml_dtypes.bfloat16)
    return np.stack([hi, lo], axis=2)


def transform_tables(height, width):
    u_half, v_half = height // 2, width // 2
    pixels = height * width
    p = np.arange(2)[:, None, None, None, None, None]
    q = np.arange(2)[:, None, None, None, None]
    u = np.arange(u_half)[:, None, None, None]
    v = np.arange(v_half)[:, None, None]
    h = np.arange(u_half)[:, None]
    w = np.arange(v_half)
    turns = (2 * u + p) * h / height + (2 * v + q) * w / width
    turns = turns.reshape(2, 2, u_half, v_half, u_half * v_half)
    angle = 2.0 * math.pi * turns
    table = np.stack([np.cos(angle), -np.sin(angle)], axis=3) / math.sqrt(pixels)
    table = table.reshape(2, 2, u_half, 2, v_half // ROWS, ROWS, u_half * v_half)
    forward = split_table(table)
    back = np.transpose(table, (0, 1, 6, 3, 4, 2, 5)).reshape(2, 2, u_half * v_half, 2 * u_half * v_half)
    return forward, split_table(back)


def low_rows(shape):
    return lax.broadcasted_iota(jnp.int32, shape, len(shape) - 2) < ROWS // 2


def roll_half(x):
    return pltpu.roll(x, ROWS // 2, x.ndim - 2)


def fold(quads, xs):
    for p in range(2):
        left, right = (quads[0][b] + quads[1][b] if p == 0 else quads[0][b] - quads[1][b] for b in range(2))
        for q in range(2):
            xs[p, q, 0], xs[p, q, 1] = split(left + right if q == 0 else left - right)


def forward_part(table_ref, xs, out_ref, p):
    _, _, _, units, _, pairs, _, depth = table_ref.shape
    channels = xs.shape[-1]
    groups = channels // LANES
    both = []
    for q in range(2):
        table = table_ref[p, q].reshape(-1, depth)
        value = dot_split(table, table[: table.shape[0] // 2], xs[p, q, 0], xs[p, q, 1])
        both.append(value.reshape(units, 2, pairs, ROWS, channels))
    for piece in range(2):
        for k in range(pairs):
            for group in range(groups):
                lanes = slice(group * LANES, (group + 1) * LANES)
                even, odd = (value[:, piece, k, :, lanes] for value in both)
                low = low_rows(even.shape)
                t = piece * groups + group
                out_ref[:, p, 2 * k, t] = jnp.where(low, even, roll_half(odd))
                out_ref[:, p, 2 * k + 1, t] = jnp.where(low, roll_half(even), odd)


def inverse_quads(m_ref, table_ref, bias):
    units, _, blocks, groups, _, _ = m_ref.shape
    low = low_rows((units, ROWS, LANES))
    parts = []
    for p in range(2):
        columns = [[], []]
        for group in range(groups // 2):
            rows = [[], []]
            for piece in range(2):
                for k in range(blocks // 2):
                    t = piece * (groups // 2) + group
                    first, second = m_ref[:, p, 2 * k, t], m_ref[:, p, 2 * k + 1, t]
                    even = jnp.where(low, first, roll_half(second))
                    odd = jnp.where(low, roll_half(first), second)
                    rows[0].append(even.reshape(units * ROWS, LANES))
                    rows[1].append(odd.reshape(units * ROWS, LANES))
            for q in range(2):
                columns[q].append(jnp.concatenate(rows[q], axis=0))
        for q in range(2):
            m_hi, m_lo = split(jnp.concatenate(columns[q], axis=1))
            table = table_ref[p, q].reshape(-1, m_hi.shape[0])
            parts.append(dot_split(table, table[: table.shape[0] // 2], m_hi, m_lo))
    ee, eo, oe, oo = parts
    along_w = [[ee + eo, ee - eo], [oe + oo, oe - oo]]
    quads = []
    for a in range(2):
        row = []
        for b in range(2):
            even, odd = along_w[0][b], along_w[1][b]
            row.append(jnp.maximum((even + odd if a == 0 else even - odd) + bias, 0.0))
        quads.append(row)
    return quads


def forward_kernel(x_hbm, table_hbm, out_ref, x_ref, table_ref, x_sems, table_sems, xs):
    def fetch_x(a):
        return pltpu.make_async_copy(x_hbm.at[a], x_ref.at[a], x_sems.at[a])

    def fetch_table(p):
        return pltpu.make_async_copy(table_hbm.at[p], table_ref.at[p], table_sems.at[p])

    for a in range(2):
        fetch_x(a).start()
    for p in range(2):
        fetch_table(p).start()
    for a in range(2):
        fetch_x(a).wait()
    _, h, _, w, channels = x_ref.shape
    fold([[x_ref[a, :, b].reshape(h * w, channels) for b in range(2)] for a in range(2)], xs)
    for p in range(2):
        fetch_table(p).wait()
        forward_part(table_ref, xs, out_ref, p)


def forward(x, table):
    channels = x.shape[-1]
    _, _, _, half, _, pairs, _, depth = table.shape
    out = jax.ShapeDtypeStruct((half, 2, 2 * pairs, 2 * channels // LANES, ROWS, LANES), F32)
    return pl.pallas_call(
        forward_kernel,
        in_specs=[HBM, HBM],
        out_specs=VMEM,
        out_shape=out,
        scratch_shapes=[
            pltpu.VMEM(x.shape, F32),
            pltpu.VMEM(table.shape, BF16),
            pltpu.SemaphoreType.DMA((2,)),
            pltpu.SemaphoreType.DMA((2,)),
            pltpu.VMEM((2, 2, 2, depth, channels), BF16),
        ],
        compiler_params=pltpu.CompilerParams(vmem_limit_bytes=16 << 20),
        cost_estimate=cost(6 * table.size // 2 * channels, (x, table, out)),
        name="forward_transform",
    )(*(pltpu.with_memory_space_constraint(a, pltpu.HBM) for a in (x, table)))


def inverse_kernel(layer, m_ref, table_ref, bias_ref, out_ref):
    _, h, _, w, channels = out_ref.shape
    quads = inverse_quads(m_ref, table_ref, bias_ref[layer : layer + 1, :])
    for a in range(2):
        for b in range(2):
            out_ref[a, :, b] = quads[a][b].reshape(h, w, channels)


def inverse(m, table, bias, layer, shape):
    out = jax.ShapeDtypeStruct(shape, F32)
    return pl.pallas_call(
        functools.partial(inverse_kernel, layer),
        in_specs=[VMEM] * 3,
        out_specs=VMEM,
        out_shape=out,
        compiler_params=pltpu.CompilerParams(vmem_limit_bytes=16 << 20),
        cost_estimate=cost(table.size // 2 * shape[-1], (m, table, out)),
        name="inverse_transform",
    )(m, table, bias)


def turn_kernel(layer, m_ref, back_ref, bias_ref, table_ref, out_ref, xs):
    fold(inverse_quads(m_ref, back_ref, bias_ref[layer : layer + 1, :]), xs)
    for p in range(2):
        forward_part(table_ref, xs, out_ref, p)


def turn(m, back_table, bias, layer, table):
    channels = bias.shape[1]
    return pl.pallas_call(
        functools.partial(turn_kernel, layer),
        in_specs=[VMEM] * 4,
        out_specs=VMEM,
        out_shape=jax.ShapeDtypeStruct(m.shape, F32),
        scratch_shapes=[pltpu.VMEM((2, 2, 2, table.shape[-1], channels), BF16)],
        compiler_params=pltpu.CompilerParams(vmem_limit_bytes=16 << 20),
        cost_estimate=cost(table.size * channels, (m, back_table, table, m)),
        name="turn",
    )(m, back_table, bias, table)


def mix_kernel(layer, v_ref, a_ref, out_ref, vs, ys):
    images, groups, per, _ = v_ref.shape
    for t in range(groups):
        hi, lo = split(jnp.transpose(v_ref[:, t], (1, 0, 2)))
        lanes = slice(t * LANES, (t + 1) * LANES)
        vs[:, :images, lanes] = hi
        vs[:, images:, lanes] = lo
    for s in range(per):
        i = 2 * s if s < per // 2 else 2 * s - per + 1
        a_hi, a_lo = split(a_ref[layer, i])
        both = dot_nt(vs[s], a_hi)
        value = both[:images] + both[images:] + dot_nt(vs[s, :images], a_lo)
        for t in range(groups):
            ys[t, s] = value[:, t * LANES : (t + 1) * LANES]
    for t in range(groups):
        out_ref[:, t] = jnp.transpose(ys[t], (1, 0, 2))


def mix(v, blocks, layer):
    images, groups, per, _ = v.shape
    both = blocks.shape[-1]
    return pl.pallas_call(
        functools.partial(mix_kernel, layer),
        in_specs=[VMEM, VMEM],
        out_specs=VMEM,
        out_shape=jax.ShapeDtypeStruct(v.shape, F32),
        scratch_shapes=[
            pltpu.VMEM((per, 2 * images, both), BF16),
            pltpu.VMEM((groups, per, images, LANES), F32),
        ],
        compiler_params=pltpu.CompilerParams(vmem_limit_bytes=16 << 20),
        cost_estimate=cost(v.size * both, (v, v, blocks)),
        name="mix",
    )(v, blocks)


def body(images, blocks, bias):
    _, channels, height, width = images.shape
    pixels = height * width
    table, back_table = (jnp.asarray(t) for t in transform_tables(height, width))

    def exchange(value):
        return lax.all_to_all(value, ("gx", "gy"), split_axis=0, concat_axis=0, tiled=True)

    sent = (lax.axis_size(("gx", "gy")), 2 * channels // LANES, ROWS, LANES)
    quads = (2, height // 2, 2, width // 2, channels)

    def mixed(v, layer):
        held = exchange(v.reshape(sent))
        return exchange(mix(held, blocks, layer)).reshape(v.shape)

    x = images.reshape(channels, pixels).T.reshape(quads)
    m = mixed(forward(x, table), 0)
    m = mixed(turn(m, back_table, bias, 0, table), 1)
    out = inverse(m, back_table, bias, 1, quads)
    return out.reshape(pixels, channels).T.reshape(1, channels, height, width)


def solution(mesh):
    placed = (P(("gx", "gy"), None, None, None), P(None, ("gx", "gy"), None, None), P())
    return jax.shard_map(
        body,
        mesh=mesh,
        in_specs=placed,
        out_specs=P(("gx", "gy"), None, None, None),
        check_vma=False,
    )
```

```python
import functools
import math

import jax
import jax.numpy as jnp
import ml_dtypes
import numpy as np
from jax import lax
from jax.experimental import pallas as pl
from jax.experimental.pallas import tpu as pltpu
from jax.sharding import PartitionSpec as P

BF16 = jnp.bfloat16
F32 = jnp.float32
LANES = 128
ROWS = 8
VMEM = pl.BlockSpec(memory_space=pltpu.VMEM)
HBM = pl.BlockSpec(memory_space=pl.ANY)


def cost(products, arrays):
    bytes_accessed = sum(math.prod(a.shape) * a.dtype.itemsize for a in arrays)
    return pl.CostEstimate(flops=6 * products, bytes_accessed=bytes_accessed, transcendentals=0)


def dot(a, b):
    return jnp.dot(a, b, preferred_element_type=F32)


def dot_nt(a, b):
    return lax.dot_general(a, b, (((1,), (1,)), ((), ())), preferred_element_type=F32)


def split(x):
    hi = x.astype(BF16)
    lo = (x - hi.astype(F32)).astype(BF16)
    return hi, lo


def dot_split(left_both, left_hi, right_hi, right_lo):
    both = dot(left_both, right_hi)
    rows = left_hi.shape[0]
    return both[:rows] + both[rows:] + dot(left_hi, right_lo)


def split_table(table):
    hi = table.astype(ml_dtypes.bfloat16)
    lo = (table - hi.astype(np.float64)).astype(ml_dtypes.bfloat16)
    return hi, lo


def primary(p, units):
    return units // 2 + 1 - p


def order(s, mirrored):
    i = 2 * s if s < ROWS // 2 else 2 * s - ROWS + 1
    return (ROWS - i) % ROWS if mirrored else i


def transform_tables(height, width):
    u_half, v_half = height // 2, width // 2
    pixels = height * width
    parity = np.arange(2)[:, None, None, None]
    u = 2 * np.arange(u_half)[:, None, None] + parity
    v = 2 * np.arange(v_half)[:, None, None] + parity
    h = np.arange(u_half)[:, None]
    w = np.arange(v_half)
    depth = u_half * v_half
    along_h = 2.0 * math.pi * np.broadcast_to(u * h / height, (2, u_half, u_half, v_half)).reshape(2, u_half, depth)
    along_w = 2.0 * math.pi * np.broadcast_to(v * w / width, (2, v_half, u_half, v_half)).reshape(2, v_half, depth)
    scale = 1.0 / math.sqrt(pixels)
    along_u = np.stack([np.cos(along_h), -np.sin(along_h)], axis=1) * scale
    along_v = np.stack([np.cos(along_w), -np.sin(along_w)], axis=1)
    factors = np.stack([along_u, along_v]).astype(np.float32)
    angle = along_h[:, None, :, None] + along_w[None, :, None, :]
    table = np.stack([np.cos(angle), -np.sin(angle)], axis=3) * scale
    forward, inverse = [], []
    for p in range(2):
        count = primary(p, u_half)
        rows = table[p, :, :count].reshape(2, count * 2 * v_half, depth)
        forward.append(np.concatenate(split_table(rows), axis=1))
        units = u_half if p == 0 else count
        back = np.zeros((2, depth, 2, v_half // ROWS, units, ROWS))
        for q in range(2):
            for unit in range(units):
                for s in range(ROWS):
                    half = ROWS // 2
                    i = order(s % half + q * half, unit >= count)
                    for k in range(v_half // ROWS):
                        at = ROWS * (2 * k + s // half) + i
                        back[q, :, :, k, unit, s] = table[p, q, unit, :, at // 2].T
        inverse.append(np.concatenate(split_table(back.reshape(2, depth, -1)), axis=1))
    return factors, forward, inverse


def low_rows(shape, rows):
    return lax.broadcasted_iota(jnp.int32, shape, len(shape) - 2) < rows


def roll_half(x):
    return pltpu.roll(x, ROWS // 2, x.ndim - 2)


def fold(quads, xs):
    for p in range(2):
        left, right = (quads[0][b] + quads[1][b] if p == 0 else quads[0][b] - quads[1][b] for b in range(2))
        for q in range(2):
            xs[p, q, 0], xs[p, q, 1] = split(left + right if q == 0 else left - right)


def mirror(tiles, vb, low):
    return jnp.where(low, tiles[-vb % len(tiles)], tiles[len(tiles) - 1 - vb])


def forward_part(table_ref, xs, out_ref, p):
    units, _, blocks, _, _, _ = out_ref.shape
    channels = xs.shape[-1]
    groups = channels // LANES
    count = primary(p, units)
    both = []
    for q in range(2):
        table = table_ref[q]
        value = dot_split(table, table[: table.shape[0] // 2], xs[p, q, 0], xs[p, q, 1])
        both.append(value.reshape(count, 2, blocks // 2, ROWS, channels))
    low = low_rows((count, ROWS, LANES), ROWS // 2)
    first = low_rows((count, ROWS, LANES), 1)
    for piece in range(2):
        for group in range(groups):
            lanes = slice(group * LANES, (group + 1) * LANES)
            t = piece * groups + group
            tiles = []
            for k in range(blocks // 2):
                even, odd = (value[:, piece, k, :, lanes] for value in both)
                tiles.append(jnp.where(low, even, roll_half(odd)))
                tiles.append(jnp.where(low, roll_half(even), odd))
            for vb in range(blocks):
                out_ref[:count, p, vb, t] = tiles[vb]
                mirrored = mirror(tiles, vb, first)
                if piece == 1:
                    mirrored = -mirrored
                for unit in range(count, units):
                    out_ref[unit, p, vb, t] = mirrored[units - p - unit]


def gather_parity(m_ref, p, t):
    units, _, blocks, groups, _, _ = m_ref.shape
    if p == 0:
        tiles = [m_ref[:, 0, vb, t] for vb in range(blocks)]
    else:
        units = primary(1, units)
        first = low_rows((units, ROWS, LANES), 1)
        turned = [
            jnp.stack([m_ref[2 * units - 1 - unit, 1, vb, t] for unit in range(units)]) for vb in range(blocks)
        ]
        tiles = []
        for vb in range(blocks):
            own, other = m_ref[:units, 1, vb, t], mirror(turned, vb, first)
            tiles.append(own + other if t < groups // 2 else own - other)
    low = low_rows(tiles[0].shape, ROWS // 2)
    evens, odds = [], []
    for k in range(blocks // 2):
        one, two = tiles[2 * k], tiles[2 * k + 1]
        evens.append(jnp.where(low, one, roll_half(two)).reshape(units * ROWS, LANES))
        odds.append(jnp.where(low, roll_half(one), two).reshape(units * ROWS, LANES))
    return evens, odds


def inverse_quads(m_ref, table_refs, bias):
    groups = m_ref.shape[3]
    parts = []
    for p in range(2):
        columns = [[], []]
        for group in range(groups // 2):
            real = gather_parity(m_ref, p, group)
            imag = gather_parity(m_ref, p, groups // 2 + group)
            for q in range(2):
                columns[q].append(jnp.concatenate(real[q] + imag[q], axis=0))
        for q in range(2):
            m_hi, m_lo = split(jnp.concatenate(columns[q], axis=1))
            table = table_refs[p][q]
            parts.append(dot_split(table, table[: table.shape[0] // 2], m_hi, m_lo))
    ee, eo, oe, oo = parts
    along_w = [[ee + eo, ee - eo], [oe + oo, oe - oo]]
    quads = []
    for a in range(2):
        row = []
        for b in range(2):
            even, odd = along_w[0][b], along_w[1][b]
            row.append(jnp.maximum((even + odd if a == 0 else even - odd) + bias, 0.0))
        quads.append(row)
    return quads


def forward_kernel(x_hbm, factors_hbm, out_ref, x_ref, factors_ref, sems, factor_sem, even_ref, odd_ref, xs):
    fetch_factors = pltpu.make_async_copy(factors_hbm, factors_ref, factor_sem)

    def fetch_x(a):
        return pltpu.make_async_copy(x_hbm.at[a], x_ref.at[a], sems.at[a])

    fetch_factors.start()
    for a in range(2):
        fetch_x(a).start()
    fetch_factors.wait()
    units = factors_ref.shape[3]
    tables = (even_ref, odd_ref)
    for p in range(2):
        count = primary(p, units)
        for q in range(2):
            cos_v, sin_v = factors_ref[1, q, 0], factors_ref[1, q, 1]
            for u in range(count):
                cos_u = factors_ref[0, p, 0, u : u + 1, :]
                sin_u = factors_ref[0, p, 1, u : u + 1, :]
                real = cos_u * cos_v - sin_u * sin_v
                imag = sin_u * cos_v + cos_u * sin_v
                hi, lo = split(jnp.concatenate([real, imag], axis=0))
                rows = 2 * units
                tables[p][q, u * rows : (u + 1) * rows] = hi
                tables[p][q, (count + u) * rows : (count + u + 1) * rows] = lo
    for a in range(2):
        fetch_x(a).wait()
    _, h, _, w, channels = x_ref.shape
    fold([[x_ref[a, :, b].reshape(h * w, channels) for b in range(2)] for a in range(2)], xs)
    for p in range(2):
        forward_part(tables[p], xs, out_ref, p)


def forward(x, factors, tables):
    _, h, _, w, channels = x.shape
    out = jax.ShapeDtypeStruct((h, 2, 2 * w // ROWS, 2 * channels // LANES, ROWS, LANES), F32)
    return pl.pallas_call(
        forward_kernel,
        in_specs=[HBM, HBM],
        out_specs=VMEM,
        out_shape=out,
        scratch_shapes=[
            pltpu.VMEM(x.shape, F32),
            pltpu.VMEM(factors.shape, F32),
            pltpu.SemaphoreType.DMA((2,)),
            pltpu.SemaphoreType.DMA,
            *(pltpu.VMEM(t.shape, BF16) for t in tables),
            pltpu.VMEM((2, 2, 2, h * w, channels), BF16),
        ],
        compiler_params=pltpu.CompilerParams(vmem_limit_bytes=16 << 20),
        cost_estimate=cost(12 * sum(t.size for t in tables) // 2 * channels, (x, factors, out)),
        name="forward_transform",
    )(*(pltpu.with_memory_space_constraint(a, pltpu.HBM) for a in (x, factors)))


def inverse_kernel(layer, m_ref, even_ref, odd_ref, bias_ref, out_ref):
    _, h, _, w, channels = out_ref.shape
    quads = inverse_quads(m_ref, (even_ref, odd_ref), bias_ref[layer : layer + 1, :])
    for a in range(2):
        for b in range(2):
            out_ref[a, :, b] = quads[a][b].reshape(h, w, channels)


def inverse(m, tables, bias, layer, shape):
    out = jax.ShapeDtypeStruct(shape, F32)
    return pl.pallas_call(
        functools.partial(inverse_kernel, layer),
        in_specs=[VMEM] * 4,
        out_specs=VMEM,
        out_shape=out,
        compiler_params=pltpu.CompilerParams(vmem_limit_bytes=16 << 20),
        cost_estimate=cost(sum(t.size for t in tables) // 2 * shape[-1], (m, *tables, out)),
        name="inverse_transform",
    )(m, *tables, bias)


def turn_kernel(layer, m_ref, back_even, back_odd, bias_ref, even_ref, odd_ref, out_ref, xs):
    fold(inverse_quads(m_ref, (back_even, back_odd), bias_ref[layer : layer + 1, :]), xs)
    for p, table_ref in enumerate((even_ref, odd_ref)):
        forward_part(table_ref, xs, out_ref, p)


def turn(m, back_tables, bias, layer, tables):
    channels = bias.shape[1]
    return pl.pallas_call(
        functools.partial(turn_kernel, layer),
        in_specs=[VMEM] * 6,
        out_specs=VMEM,
        out_shape=jax.ShapeDtypeStruct(m.shape, F32),
        scratch_shapes=[pltpu.VMEM((2, 2, 2, tables[0].shape[-1], channels), BF16)],
        compiler_params=pltpu.CompilerParams(vmem_limit_bytes=16 << 20),
        cost_estimate=cost(sum(t.size for t in (*back_tables, *tables)) // 2 * channels, (m, *back_tables, *tables, m)),
        name="turn",
    )(m, *back_tables, bias, *tables)


def mix_kernel(layer, is_mirrored, v_ref, a_ref, out_ref, vs, ys):
    images, groups, per, _ = v_ref.shape
    for t in range(groups):
        hi, lo = split(jnp.transpose(v_ref[:, t], (1, 0, 2)))
        lanes = slice(t * LANES, (t + 1) * LANES)
        vs[:, :images, lanes] = hi
        vs[:, images:, lanes] = lo
    mirrored = is_mirrored()
    for s in range(per):
        i = jnp.where(mirrored, order(s, True), order(s, False))
        a_hi, a_lo = split(a_ref[layer, i])
        both = dot_nt(vs[s], a_hi)
        value = both[:images] + both[images:] + dot_nt(vs[s, :images], a_lo)
        for t in range(groups):
            ys[t, s] = value[:, t * LANES : (t + 1) * LANES]
    for t in range(groups):
        out_ref[:, t] = jnp.transpose(ys[t], (1, 0, 2))


def mix(v, blocks, layer, is_mirrored):
    images, groups, per, _ = v.shape
    both = blocks.shape[-1]
    return pl.pallas_call(
        functools.partial(mix_kernel, layer, is_mirrored),
        in_specs=[VMEM, VMEM],
        out_specs=VMEM,
        out_shape=jax.ShapeDtypeStruct(v.shape, F32),
        scratch_shapes=[
            pltpu.VMEM((per, 2 * images, both), BF16),
            pltpu.VMEM((groups, per, images, LANES), F32),
        ],
        compiler_params=pltpu.CompilerParams(vmem_limit_bytes=16 << 20),
        cost_estimate=cost(v.size * both, (v, v, blocks)),
        name="mix",
    )(v, blocks)


def body(images, blocks, bias):
    _, channels, height, width = images.shape
    pixels = height * width
    factors, tables, back_tables = jax.tree.map(jnp.asarray, transform_tables(height, width))

    def exchange(value):
        return lax.all_to_all(value, ("gx", "gy"), split_axis=0, concat_axis=0, tiled=True)

    sent = (lax.axis_size(("gx", "gy")), 2 * channels // LANES, ROWS, LANES)
    quads = (2, height // 2, 2, width // 2, channels)

    def is_mirrored():
        u = (lax.axis_index("gx") * lax.axis_size("gy") + lax.axis_index("gy")) // (width // ROWS)
        return u > height // 2

    def mixed(v, layer):
        held = exchange(v.reshape(sent))
        return exchange(mix(held, blocks, layer, is_mirrored)).reshape(v.shape)

    x = images.reshape(channels, pixels).T.reshape(quads)
    m = mixed(forward(x, factors, tables), 0)
    m = mixed(turn(m, back_tables, bias, 0, tables), 1)
    out = inverse(m, back_tables, bias, 1, quads)
    return out.reshape(pixels, channels).T.reshape(1, channels, height, width)


def solution(mesh):
    placed = (P(("gx", "gy"), None, None, None), P(None, ("gx", "gy"), None, None), P())
    return jax.shard_map(
        body,
        mesh=mesh,
        in_specs=placed,
        out_specs=P(("gx", "gy"), None, None, None),
        check_vma=False,
    )
```

```python
import functools
import math

import jax
import jax.numpy as jnp
import ml_dtypes
import numpy as np
from jax import lax
from jax.experimental import pallas as pl
from jax.experimental.pallas import tpu as pltpu
from jax.sharding import PartitionSpec as P

BF16 = jnp.bfloat16
F32 = jnp.float32
LANES = 128
ROWS = 8
VMEM = pl.BlockSpec(memory_space=pltpu.VMEM)
HBM = pl.BlockSpec(memory_space=pl.ANY)


def cost(products, arrays):
    bytes_accessed = sum(math.prod(a.shape) * a.dtype.itemsize for a in arrays)
    return pl.CostEstimate(flops=6 * products, bytes_accessed=bytes_accessed, transcendentals=0)


def dot(a, b):
    return jnp.dot(a, b, preferred_element_type=F32)


def dot_nt(a, b):
    return lax.dot_general(a, b, (((1,), (1,)), ((), ())), preferred_element_type=F32)


def split(x):
    hi = x.astype(BF16)
    lo = (x - hi.astype(F32)).astype(BF16)
    return hi, lo


def dot_split(left_both, left_hi, right_hi, right_lo):
    both = dot(left_both, right_hi)
    rows = left_hi.shape[0]
    return both[:rows] + both[rows:] + dot(left_hi, right_lo)


def split_table(table):
    hi = table.astype(ml_dtypes.bfloat16)
    lo = (table - hi.astype(np.float64)).astype(ml_dtypes.bfloat16)
    return hi, lo


def primary(p, units):
    return units // 2 + 1 - p


def order(s, mirrored):
    i = 2 * s if s < ROWS // 2 else 2 * s - ROWS + 1
    return (ROWS - i) % ROWS if mirrored else i


def transform_tables(height, width):
    u_half, v_half = height // 2, width // 2
    pixels = height * width
    parity = np.arange(2)[:, None, None, None]
    u = 2 * np.arange(u_half)[:, None, None] + parity
    v = 2 * np.arange(v_half)[:, None, None] + parity
    h = np.arange(u_half)[:, None]
    w = np.arange(v_half)
    depth = u_half * v_half
    along_h = 2.0 * math.pi * np.broadcast_to(u * h / height, (2, u_half, u_half, v_half)).reshape(2, u_half, depth)
    along_w = 2.0 * math.pi * np.broadcast_to(v * w / width, (2, v_half, u_half, v_half)).reshape(2, v_half, depth)
    scale = 1.0 / math.sqrt(pixels)
    along_u = np.stack([np.cos(along_h), -np.sin(along_h)], axis=1) * scale
    along_v = np.stack([np.cos(along_w), -np.sin(along_w)], axis=1)
    factors = np.stack([along_u, along_v]).astype(np.float32)
    angle = along_h[:, None, :, None] + along_w[None, :, None, :]
    table = np.stack([np.cos(angle), -np.sin(angle)], axis=3) * scale
    forward, inverse = [], []
    for p in range(2):
        count = primary(p, u_half)
        rows = table[p, :, :count].reshape(2, count * 2 * v_half, depth)
        forward.append(np.concatenate(split_table(rows), axis=1))
        back = table[p, :, : u_half // 2].reshape(2, u_half // 2, 2, v_half // ROWS, ROWS, depth)
        back = np.transpose(back, (0, 5, 2, 3, 1, 4)).reshape(2, depth, -1)
        inverse.append(np.concatenate(split_table(back), axis=1))
    middle = np.transpose(table[0, :, u_half // 2, :, :, :v_half], (0, 3, 1, 2)).reshape(2, v_half, 2 * v_half)
    inverse.append(np.concatenate(split_table(middle), axis=1))
    return factors, forward, inverse


def low_rows(shape, rows):
    return lax.broadcasted_iota(jnp.int32, shape, len(shape) - 2) < rows


def roll_half(x):
    return pltpu.roll(x, ROWS // 2, x.ndim - 2)


def fold(quads, xs):
    for p in range(2):
        left, right = (quads[0][b] + quads[1][b] if p == 0 else quads[0][b] - quads[1][b] for b in range(2))
        for q in range(2):
            xs[p, q, 0], xs[p, q, 1] = split(left + right if q == 0 else left - right)


def mirror(tiles, vb, low):
    return jnp.where(low, tiles[-vb % len(tiles)], tiles[len(tiles) - 1 - vb])


def forward_part(table_ref, xs, out_ref, p):
    units, _, blocks, _, _, _ = out_ref.shape
    channels = xs.shape[-1]
    groups = channels // LANES
    count = primary(p, units)
    both = []
    for q in range(2):
        table = table_ref[q]
        value = dot_split(table, table[: table.shape[0] // 2], xs[p, q, 0], xs[p, q, 1])
        both.append(value.reshape(count, 2, blocks // 2, ROWS, channels))
    low = low_rows((count, ROWS, LANES), ROWS // 2)
    first = low_rows((count, ROWS, LANES), 1)
    for piece in range(2):
        for group in range(groups):
            lanes = slice(group * LANES, (group + 1) * LANES)
            t = piece * groups + group
            tiles = []
            for k in range(blocks // 2):
                even, odd = (value[:, piece, k, :, lanes] for value in both)
                tiles.append(jnp.where(low, even, roll_half(odd)))
                tiles.append(jnp.where(low, roll_half(even), odd))
            for vb in range(blocks):
                out_ref[:count, p, vb, t] = tiles[vb]
                mirrored = mirror(tiles, vb, first)
                if piece == 1:
                    mirrored = -mirrored
                for unit in range(count, units):
                    out_ref[unit, p, vb, t] = mirrored[units - p - unit]


def join_parities(tiles):
    low = low_rows(tiles[0].shape, ROWS // 2)
    rows = tiles[0].shape[0] * ROWS
    evens, odds = [], []
    for k in range(len(tiles) // 2):
        one, two = tiles[2 * k], tiles[2 * k + 1]
        evens.append(jnp.where(low, one, roll_half(two)).reshape(rows, LANES))
        odds.append(jnp.where(low, roll_half(one), two).reshape(rows, LANES))
    return evens, odds


def gather_parity(m_ref, p, t):
    units, _, blocks, groups, _, _ = m_ref.shape
    half = units // 2
    first = low_rows((half, ROWS, LANES), 1)
    turned = []
    for vb in range(blocks):
        others = [m_ref[units - p - unit, p, vb, t] for unit in range(1 - p, half)]
        if p == 0:
            others.insert(0, jnp.zeros_like(others[0]))
        turned.append(jnp.stack(others))
    tiles = []
    for vb in range(blocks):
        own, other = m_ref[:half, p, vb, t], mirror(turned, vb, first)
        tiles.append(own + other if t < groups // 2 else own - other)
    return join_parities(tiles)


def gather_middle(m_ref, p, t):
    half = m_ref.shape[0] // 2
    return join_parities([m_ref[half : half + 1, p, vb, t] for vb in range(m_ref.shape[2])])


def product(gather, m_ref, p, table_ref):
    groups = m_ref.shape[3]
    columns = [[], []]
    for group in range(groups // 2):
        real = gather(m_ref, p, group)
        imag = gather(m_ref, p, groups // 2 + group)
        for q in range(2):
            columns[q].append(jnp.concatenate(real[q] + imag[q], axis=0))
    values = []
    for q in range(2):
        m_hi, m_lo = split(jnp.concatenate(columns[q], axis=1))
        table = table_ref[q]
        values.append(dot_split(table, table[: table.shape[0] // 2], m_hi, m_lo))
    return values


def inverse_quads(m_ref, table_refs, bias):
    even_ref, odd_ref, middle_ref = table_refs
    parts = product(gather_parity, m_ref, 0, even_ref) + product(gather_parity, m_ref, 1, odd_ref)
    for q, value in enumerate(product(gather_middle, m_ref, 0, middle_ref)):
        repeats = parts[q].shape[0] // (2 * value.shape[0])
        parts[q] += jnp.concatenate([value, -value] * repeats, axis=0)
    ee, eo, oe, oo = parts
    along_w = [[ee + eo, ee - eo], [oe + oo, oe - oo]]
    quads = []
    for a in range(2):
        row = []
        for b in range(2):
            even, odd = along_w[0][b], along_w[1][b]
            row.append(jnp.maximum((even + odd if a == 0 else even - odd) + bias, 0.0))
        quads.append(row)
    return quads


def forward_kernel(x_hbm, factors_hbm, out_ref, x_ref, factors_ref, sems, factor_sem, even_ref, odd_ref, xs):
    fetch_factors = pltpu.make_async_copy(factors_hbm, factors_ref, factor_sem)

    def fetch_x(a):
        return pltpu.make_async_copy(x_hbm.at[a], x_ref.at[a], sems.at[a])

    fetch_factors.start()
    for a in range(2):
        fetch_x(a).start()
    fetch_factors.wait()
    units = factors_ref.shape[3]
    tables = (even_ref, odd_ref)
    for p in range(2):
        count = primary(p, units)
        for q in range(2):
            cos_v, sin_v = factors_ref[1, q, 0], factors_ref[1, q, 1]
            for u in range(count):
                cos_u = factors_ref[0, p, 0, u : u + 1, :]
                sin_u = factors_ref[0, p, 1, u : u + 1, :]
                real = cos_u * cos_v - sin_u * sin_v
                imag = sin_u * cos_v + cos_u * sin_v
                hi, lo = split(jnp.concatenate([real, imag], axis=0))
                rows = 2 * units
                tables[p][q, u * rows : (u + 1) * rows] = hi
                tables[p][q, (count + u) * rows : (count + u + 1) * rows] = lo
    for a in range(2):
        fetch_x(a).wait()
    _, h, _, w, channels = x_ref.shape
    fold([[x_ref[a, :, b].reshape(h * w, channels) for b in range(2)] for a in range(2)], xs)
    for p in range(2):
        forward_part(tables[p], xs, out_ref, p)


def forward(x, factors, tables):
    _, h, _, w, channels = x.shape
    out = jax.ShapeDtypeStruct((h, 2, 2 * w // ROWS, 2 * channels // LANES, ROWS, LANES), F32)
    return pl.pallas_call(
        forward_kernel,
        in_specs=[HBM, HBM],
        out_specs=VMEM,
        out_shape=out,
        scratch_shapes=[
            pltpu.VMEM(x.shape, F32),
            pltpu.VMEM(factors.shape, F32),
            pltpu.SemaphoreType.DMA((2,)),
            pltpu.SemaphoreType.DMA,
            *(pltpu.VMEM(t.shape, BF16) for t in tables),
            pltpu.VMEM((2, 2, 2, h * w, channels), BF16),
        ],
        compiler_params=pltpu.CompilerParams(vmem_limit_bytes=16 << 20),
        cost_estimate=cost(12 * sum(t.size for t in tables) // 2 * channels, (x, factors, out)),
        name="forward_transform",
    )(*(pltpu.with_memory_space_constraint(a, pltpu.HBM) for a in (x, factors)))


def inverse_kernel(layer, m_ref, even_ref, odd_ref, middle_ref, bias_ref, out_ref):
    _, h, _, w, channels = out_ref.shape
    quads = inverse_quads(m_ref, (even_ref, odd_ref, middle_ref), bias_ref[layer : layer + 1, :])
    for a in range(2):
        for b in range(2):
            out_ref[a, :, b] = quads[a][b].reshape(h, w, channels)


def inverse(m, tables, bias, layer, shape):
    out = jax.ShapeDtypeStruct(shape, F32)
    return pl.pallas_call(
        functools.partial(inverse_kernel, layer),
        in_specs=[VMEM] * 5,
        out_specs=VMEM,
        out_shape=out,
        compiler_params=pltpu.CompilerParams(vmem_limit_bytes=16 << 20),
        cost_estimate=cost(sum(t.size for t in tables) // 2 * shape[-1], (m, *tables, out)),
        name="inverse_transform",
    )(m, *tables, bias)


def turn_kernel(layer, m_ref, back_even, back_odd, back_middle, bias_ref, even_ref, odd_ref, out_ref, xs):
    fold(inverse_quads(m_ref, (back_even, back_odd, back_middle), bias_ref[layer : layer + 1, :]), xs)
    for p, table_ref in enumerate((even_ref, odd_ref)):
        forward_part(table_ref, xs, out_ref, p)


def turn(m, back_tables, bias, layer, tables):
    channels = bias.shape[1]
    return pl.pallas_call(
        functools.partial(turn_kernel, layer),
        in_specs=[VMEM] * 7,
        out_specs=VMEM,
        out_shape=jax.ShapeDtypeStruct(m.shape, F32),
        scratch_shapes=[pltpu.VMEM((2, 2, 2, tables[0].shape[-1], channels), BF16)],
        compiler_params=pltpu.CompilerParams(vmem_limit_bytes=16 << 20),
        cost_estimate=cost(sum(t.size for t in (*back_tables, *tables)) // 2 * channels, (m, *back_tables, *tables, m)),
        name="turn",
    )(m, *back_tables, bias, *tables)


def mix_kernel(layer, is_mirrored, v_ref, a_ref, out_ref, vs, ys):
    images, groups, per, _ = v_ref.shape
    for t in range(groups):
        hi, lo = split(jnp.transpose(v_ref[:, t], (1, 0, 2)))
        lanes = slice(t * LANES, (t + 1) * LANES)
        vs[:, :images, lanes] = hi
        vs[:, images:, lanes] = lo
    mirrored = is_mirrored()
    for s in range(per):
        i = jnp.where(mirrored, order(s, True), order(s, False))
        a_hi, a_lo = split(a_ref[layer, i])
        both = dot_nt(vs[s], a_hi)
        low_part = dot_nt(a_lo, vs[s, :images])
        for t in range(groups):
            lanes = slice(t * LANES, (t + 1) * LANES)
            ys[t, s] = both[:images, lanes] + both[images:, lanes] + low_part[lanes].T
    for t in range(groups):
        out_ref[:, t] = jnp.transpose(ys[t], (1, 0, 2))


def mix(v, blocks, layer, is_mirrored):
    images, groups, per, _ = v.shape
    both = blocks.shape[-1]
    return pl.pallas_call(
        functools.partial(mix_kernel, layer, is_mirrored),
        in_specs=[VMEM, VMEM],
        out_specs=VMEM,
        out_shape=jax.ShapeDtypeStruct(v.shape, F32),
        scratch_shapes=[
            pltpu.VMEM((per, 2 * images, both), BF16),
            pltpu.VMEM((groups, per, images, LANES), F32),
        ],
        compiler_params=pltpu.CompilerParams(vmem_limit_bytes=16 << 20),
        cost_estimate=cost(v.size * both, (v, v, blocks)),
        name="mix",
    )(v, blocks)


def body(images, blocks, bias):
    _, channels, height, width = images.shape
    pixels = height * width
    factors, tables, back_tables = jax.tree.map(jnp.asarray, transform_tables(height, width))

    def exchange(value):
        return lax.all_to_all(value, ("gx", "gy"), split_axis=0, concat_axis=0, tiled=True)

    sent = (lax.axis_size(("gx", "gy")), 2 * channels // LANES, ROWS, LANES)
    quads = (2, height // 2, 2, width // 2, channels)

    def is_mirrored():
        u = (lax.axis_index("gx") * lax.axis_size("gy") + lax.axis_index("gy")) // (width // ROWS)
        return u > height // 2

    def mixed(v, layer):
        held = exchange(v.reshape(sent))
        return exchange(mix(held, blocks, layer, is_mirrored)).reshape(v.shape)

    x = images.reshape(channels, pixels).T.reshape(quads)
    m = mixed(forward(x, factors, tables), 0)
    m = mixed(turn(m, back_tables, bias, 0, tables), 1)
    out = inverse(m, back_tables, bias, 1, quads)
    return out.reshape(pixels, channels).T.reshape(1, channels, height, width)


def solution(mesh):
    placed = (P(("gx", "gy"), None, None, None), P(None, ("gx", "gy"), None, None), P())
    return jax.shard_map(
        body,
        mesh=mesh,
        in_specs=placed,
        out_specs=P(("gx", "gy"), None, None, None),
        check_vma=False,
    )
```

```python
import functools
import math

import jax
import jax.numpy as jnp
import ml_dtypes
import numpy as np
from jax import lax
from jax.experimental import pallas as pl
from jax.experimental.pallas import tpu as pltpu
from jax.sharding import PartitionSpec as P

BF16 = jnp.bfloat16
F32 = jnp.float32
LANES = 128
ROWS = 8
VMEM = pl.BlockSpec(memory_space=pltpu.VMEM)
HBM = pl.BlockSpec(memory_space=pl.ANY)


def cost(products, arrays):
    bytes_accessed = sum(math.prod(a.shape) * a.dtype.itemsize for a in arrays)
    return pl.CostEstimate(flops=6 * products, bytes_accessed=bytes_accessed, transcendentals=0)


def dot(a, b):
    return jnp.dot(a, b, preferred_element_type=F32)


def dot_nt(a, b):
    return lax.dot_general(a, b, (((1,), (1,)), ((), ())), preferred_element_type=F32)


def split(x):
    hi = x.astype(BF16)
    lo = (x - hi.astype(F32)).astype(BF16)
    return hi, lo


def dot_split(left_both, left_hi, right_hi, right_lo):
    both = dot(left_both, right_hi)
    rows = left_hi.shape[0]
    return both[:rows] + both[rows:] + dot(left_hi, right_lo)


def split_table(table):
    hi = table.astype(ml_dtypes.bfloat16)
    lo = (table - hi.astype(np.float64)).astype(ml_dtypes.bfloat16)
    return hi, lo


def primary(p, units):
    return units // 2 + 1 - p


def order(s, mirrored):
    i = 2 * s if s < ROWS // 2 else 2 * s - ROWS + 1
    return (ROWS - i) % ROWS if mirrored else i


def transform_tables(height, width):
    u_half, v_half = height // 2, width // 2
    pixels = height * width
    parity = np.arange(2)[:, None, None, None]
    u = 2 * np.arange(u_half)[:, None, None] + parity
    v = 2 * np.arange(v_half)[:, None, None] + parity
    h = np.arange(u_half)[:, None]
    w = np.arange(v_half)
    depth = u_half * v_half
    along_h = 2.0 * math.pi * np.broadcast_to(u * h / height, (2, u_half, u_half, v_half)).reshape(2, u_half, depth)
    along_w = 2.0 * math.pi * np.broadcast_to(v * w / width, (2, v_half, u_half, v_half)).reshape(2, v_half, depth)
    scale = 1.0 / math.sqrt(pixels)
    along_u = np.stack([np.cos(along_h), -np.sin(along_h)], axis=1) * scale
    along_v = np.stack([np.cos(along_w), -np.sin(along_w)], axis=1)
    factors = np.stack([along_u, along_v]).astype(np.float32)
    angle = along_h[:, None, :, None] + along_w[None, :, None, :]
    table = np.stack([np.cos(angle), -np.sin(angle)], axis=3) * scale
    forward, inverse = [], []
    for p in range(2):
        count = primary(p, u_half)
        rows = table[p, :, :count].reshape(2, count * 2 * v_half, depth)
        forward.append(np.concatenate(split_table(rows), axis=1))
        back = table[p, :, : u_half // 2].reshape(2, u_half // 2, 2, v_half // ROWS, ROWS, depth)
        back = np.transpose(back, (0, 5, 2, 3, 1, 4)).reshape(2, depth, -1)
        inverse.append(np.concatenate(split_table(back), axis=1))
    middle = np.transpose(table[0, :, u_half // 2, :, :, :v_half], (0, 3, 1, 2)).reshape(2, v_half, 2 * v_half)
    inverse.append(np.concatenate(split_table(middle), axis=1))
    return factors, forward, inverse


def low_rows(shape, rows):
    return lax.broadcasted_iota(jnp.int32, shape, len(shape) - 2) < rows


def roll_half(x):
    return pltpu.roll(x, ROWS // 2, x.ndim - 2)


def fold(quads, xs):
    for p in range(2):
        left, right = (quads[0][b] + quads[1][b] if p == 0 else quads[0][b] - quads[1][b] for b in range(2))
        for q in range(2):
            xs[p, q, 0], xs[p, q, 1] = split(left + right if q == 0 else left - right)


def mirror(tiles, vb, low):
    return jnp.where(low, tiles[-vb % len(tiles)], tiles[len(tiles) - 1 - vb])


def forward_part(table_ref, xs, out_ref, p):
    units, _, blocks, _, _, _ = out_ref.shape
    channels = xs.shape[-1]
    groups = channels // LANES
    count = primary(p, units)
    both = []
    for q in range(2):
        table = table_ref[q]
        value = dot_split(table, table[: table.shape[0] // 2], xs[p, q, 0], xs[p, q, 1])
        both.append(value.reshape(count, 2, blocks // 2, ROWS, channels))
    low = low_rows((count, ROWS, LANES), ROWS // 2)
    first = low_rows((count, ROWS, LANES), 1)
    for piece in range(2):
        for group in range(groups):
            lanes = slice(group * LANES, (group + 1) * LANES)
            t = piece * groups + group
            tiles = []
            for k in range(blocks // 2):
                even, odd = (value[:, piece, k, :, lanes] for value in both)
                tiles.append(jnp.where(low, even, roll_half(odd)))
                tiles.append(jnp.where(low, roll_half(even), odd))
            for vb in range(blocks):
                out_ref[:count, p, vb, t] = tiles[vb]
                mirrored = mirror(tiles, vb, first)
                if piece == 1:
                    mirrored = -mirrored
                for unit in range(count, units):
                    out_ref[unit, p, vb, t] = mirrored[units - p - unit]


def join_parities(tiles):
    low = low_rows(tiles[0].shape, ROWS // 2)
    rows = tiles[0].shape[0] * ROWS
    evens, odds = [], []
    for k in range(len(tiles) // 2):
        one, two = tiles[2 * k], tiles[2 * k + 1]
        evens.append(jnp.where(low, one, roll_half(two)).reshape(rows, LANES))
        odds.append(jnp.where(low, roll_half(one), two).reshape(rows, LANES))
    return evens, odds


def gather_parity(m_ref, p, t):
    units, _, blocks, groups, _, _ = m_ref.shape
    half = units // 2
    first = low_rows((half, ROWS, LANES), 1)
    turned = []
    for vb in range(blocks):
        others = [m_ref[units - p - unit, p, vb, t] for unit in range(1 - p, half)]
        if p == 0:
            others.insert(0, jnp.zeros_like(others[0]))
        turned.append(jnp.stack(others))
    tiles = []
    for vb in range(blocks):
        own, other = m_ref[:half, p, vb, t], mirror(turned, vb, first)
        tiles.append(own + other if t < groups // 2 else own - other)
    return join_parities(tiles)


def gather_middle(m_ref, p, t):
    half = m_ref.shape[0] // 2
    return join_parities([m_ref[half : half + 1, p, vb, t] for vb in range(m_ref.shape[2])])


def operands(gather, m_ref, p):
    groups = m_ref.shape[3]
    columns = [[], []]
    for group in range(groups // 2):
        real = gather(m_ref, p, group)
        imag = gather(m_ref, p, groups // 2 + group)
        for q in range(2):
            columns[q].append(jnp.concatenate(real[q] + imag[q], axis=0))
    return [split(jnp.concatenate(columns[q], axis=1)) for q in range(2)]


def product(table, pair, part=0, parts=1):
    rows = table.shape[0] // 2
    count = rows // parts
    hi = table[part * count : (part + 1) * count]
    if parts == 1:
        return dot_split(table, hi, *pair)
    lo = table[rows + part * count : rows + (part + 1) * count]
    return dot_split(jnp.concatenate([hi, lo], axis=0), hi, *pair)


def inverse_quads(m_ref, table_refs, bias, parts=1):
    even_ref, odd_ref, middle_ref = table_refs
    pairs = operands(gather_parity, m_ref, 0) + operands(gather_parity, m_ref, 1)
    middle = [product(middle_ref[q], pair) for q, pair in enumerate(operands(gather_middle, m_ref, 0))]
    for part in range(parts):
        values = [product((even_ref, odd_ref)[i // 2][i % 2], pair, part, parts) for i, pair in enumerate(pairs)]
        for q, value in enumerate(middle):
            repeats = values[q].shape[0] // (2 * value.shape[0])
            values[q] += jnp.concatenate([value, -value] * repeats, axis=0)
        yield join_quads(values, bias)


def join_quads(values, bias):
    ee, eo, oe, oo = values
    along_w = [[ee + eo, ee - eo], [oe + oo, oe - oo]]
    quads = []
    for a in range(2):
        row = []
        for b in range(2):
            even, odd = along_w[0][b], along_w[1][b]
            row.append(jnp.maximum((even + odd if a == 0 else even - odd) + bias, 0.0))
        quads.append(row)
    return quads


def forward_kernel(x_hbm, factors_hbm, out_ref, x_ref, factors_ref, sems, factor_sem, even_ref, odd_ref, xs):
    fetch_factors = pltpu.make_async_copy(factors_hbm, factors_ref, factor_sem)

    def fetch_x(a):
        return pltpu.make_async_copy(x_hbm.at[a], x_ref.at[a], sems.at[a])

    fetch_factors.start()
    for a in range(2):
        fetch_x(a).start()
    fetch_factors.wait()
    units = factors_ref.shape[3]
    tables = (even_ref, odd_ref)
    for p in range(2):
        count = primary(p, units)
        for q in range(2):
            cos_v, sin_v = factors_ref[1, q, 0], factors_ref[1, q, 1]
            for u in range(count):
                cos_u = factors_ref[0, p, 0, u : u + 1, :]
                sin_u = factors_ref[0, p, 1, u : u + 1, :]
                real = cos_u * cos_v - sin_u * sin_v
                imag = sin_u * cos_v + cos_u * sin_v
                hi, lo = split(jnp.concatenate([real, imag], axis=0))
                rows = 2 * units
                tables[p][q, u * rows : (u + 1) * rows] = hi
                tables[p][q, (count + u) * rows : (count + u + 1) * rows] = lo
    for a in range(2):
        fetch_x(a).wait()
    _, h, _, w, channels = x_ref.shape
    fold([[x_ref[a, :, b].reshape(h * w, channels) for b in range(2)] for a in range(2)], xs)
    for p in range(2):
        forward_part(tables[p], xs, out_ref, p)


def forward(x, factors, tables):
    _, h, _, w, channels = x.shape
    out = jax.ShapeDtypeStruct((h, 2, 2 * w // ROWS, 2 * channels // LANES, ROWS, LANES), F32)
    return pl.pallas_call(
        forward_kernel,
        in_specs=[HBM, HBM],
        out_specs=VMEM,
        out_shape=out,
        scratch_shapes=[
            pltpu.VMEM(x.shape, F32),
            pltpu.VMEM(factors.shape, F32),
            pltpu.SemaphoreType.DMA((2,)),
            pltpu.SemaphoreType.DMA,
            *(pltpu.VMEM(t.shape, BF16) for t in tables),
            pltpu.VMEM((2, 2, 2, h * w, channels), BF16),
        ],
        compiler_params=pltpu.CompilerParams(vmem_limit_bytes=16 << 20),
        cost_estimate=cost(12 * sum(t.size for t in tables) // 2 * channels, (x, factors, out)),
        name="forward_transform",
    )(*(pltpu.with_memory_space_constraint(a, pltpu.HBM) for a in (x, factors)))


def inverse_kernel(layer, m_ref, even_ref, odd_ref, middle_ref, bias_ref, out_hbm, out_ref, sems):
    _, h, _, w, channels = out_ref.shape
    parts = sems.shape[0]
    rows = h // parts

    def write(part, a):
        at = pl.ds(part * rows, rows)
        return pltpu.make_async_copy(out_ref.at[a, at], out_hbm.at[a, at], sems.at[part, a])

    bias = bias_ref[layer : layer + 1, :]
    for part, quads in enumerate(inverse_quads(m_ref, (even_ref, odd_ref, middle_ref), bias, parts)):
        for a in range(2):
            for b in range(2):
                out_ref[a, part * rows : (part + 1) * rows, b] = quads[a][b].reshape(rows, w, channels)
            write(part, a).start()
    for part in range(parts):
        for a in range(2):
            write(part, a).wait()


def inverse(m, tables, bias, layer, shape):
    out = jax.ShapeDtypeStruct(shape, F32)
    return pl.pallas_call(
        functools.partial(inverse_kernel, layer),
        in_specs=[VMEM] * 5,
        out_specs=HBM,
        out_shape=out,
        scratch_shapes=[pltpu.VMEM(shape, F32), pltpu.SemaphoreType.DMA((2, 2))],
        compiler_params=pltpu.CompilerParams(vmem_limit_bytes=16 << 20),
        cost_estimate=cost(sum(t.size for t in tables) // 2 * shape[-1], (m, *tables, out)),
        name="inverse_transform",
    )(m, *tables, bias)


def turn_kernel(layer, m_ref, back_even, back_odd, back_middle, bias_ref, even_ref, odd_ref, out_ref, xs):
    tables = (back_even, back_odd, back_middle)
    (quads,) = inverse_quads(m_ref, tables, bias_ref[layer : layer + 1, :])
    fold(quads, xs)
    for p, table_ref in enumerate((even_ref, odd_ref)):
        forward_part(table_ref, xs, out_ref, p)


def turn(m, back_tables, bias, layer, tables):
    channels = bias.shape[1]
    return pl.pallas_call(
        functools.partial(turn_kernel, layer),
        in_specs=[VMEM] * 7,
        out_specs=VMEM,
        out_shape=jax.ShapeDtypeStruct(m.shape, F32),
        scratch_shapes=[pltpu.VMEM((2, 2, 2, tables[0].shape[-1], channels), BF16)],
        compiler_params=pltpu.CompilerParams(vmem_limit_bytes=16 << 20),
        cost_estimate=cost(sum(t.size for t in (*back_tables, *tables)) // 2 * channels, (m, *back_tables, *tables, m)),
        name="turn",
    )(m, *back_tables, bias, *tables)


def mix_kernel(layer, is_mirrored, v_ref, a_ref, out_ref, vs, ys):
    images, groups, per, _ = v_ref.shape
    for t in range(groups):
        hi, lo = split(jnp.transpose(v_ref[:, t], (1, 0, 2)))
        lanes = slice(t * LANES, (t + 1) * LANES)
        vs[:, :images, lanes] = hi
        vs[:, images:, lanes] = lo
    mirrored = is_mirrored()
    for s in range(per):
        i = jnp.where(mirrored, order(s, True), order(s, False))
        a_hi, a_lo = split(a_ref[layer, i])
        both = dot_nt(vs[s], a_hi)
        low_part = dot_nt(a_lo, vs[s, :images])
        for t in range(groups):
            lanes = slice(t * LANES, (t + 1) * LANES)
            ys[t, s] = both[:images, lanes] + both[images:, lanes] + low_part[lanes].T
    for t in range(groups):
        out_ref[:, t] = jnp.transpose(ys[t], (1, 0, 2))


def mix(v, blocks, layer, is_mirrored):
    images, groups, per, _ = v.shape
    both = blocks.shape[-1]
    return pl.pallas_call(
        functools.partial(mix_kernel, layer, is_mirrored),
        in_specs=[VMEM, VMEM],
        out_specs=VMEM,
        out_shape=jax.ShapeDtypeStruct(v.shape, F32),
        scratch_shapes=[
            pltpu.VMEM((per, 2 * images, both), BF16),
            pltpu.VMEM((groups, per, images, LANES), F32),
        ],
        compiler_params=pltpu.CompilerParams(vmem_limit_bytes=16 << 20),
        cost_estimate=cost(v.size * both, (v, v, blocks)),
        name="mix",
    )(v, blocks)


def body(images, blocks, bias):
    _, channels, height, width = images.shape
    pixels = height * width
    factors, tables, back_tables = jax.tree.map(jnp.asarray, transform_tables(height, width))

    def exchange(value):
        return lax.all_to_all(value, ("gx", "gy"), split_axis=0, concat_axis=0, tiled=True)

    sent = (lax.axis_size(("gx", "gy")), 2 * channels // LANES, ROWS, LANES)
    quads = (2, height // 2, 2, width // 2, channels)

    def is_mirrored():
        u = (lax.axis_index("gx") * lax.axis_size("gy") + lax.axis_index("gy")) // (width // ROWS)
        return u > height // 2

    def mixed(v, layer):
        held = exchange(v.reshape(sent))
        return exchange(mix(held, blocks, layer, is_mirrored)).reshape(v.shape)

    x = images.reshape(channels, pixels).T.reshape(quads)
    m = mixed(forward(x, factors, tables), 0)
    m = mixed(turn(m, back_tables, bias, 0, tables), 1)
    out = inverse(m, back_tables, bias, 1, quads)
    return out.reshape(pixels, channels).T.reshape(1, channels, height, width)


def solution(mesh):
    placed = (P(("gx", "gy"), None, None, None), P(None, ("gx", "gy"), None, None), P())
    return jax.shard_map(
        body,
        mesh=mesh,
        in_specs=placed,
        out_specs=P(("gx", "gy"), None, None, None),
        check_vma=False,
    )
```

```python
import functools
import math

import jax
import jax.numpy as jnp
import ml_dtypes
import numpy as np
from jax import lax
from jax.experimental import pallas as pl
from jax.experimental.pallas import tpu as pltpu
from jax.sharding import PartitionSpec as P

BF16 = jnp.bfloat16
F32 = jnp.float32
LANES = 128
ROWS = 8
VMEM = pl.BlockSpec(memory_space=pltpu.VMEM)
HBM = pl.BlockSpec(memory_space=pl.ANY)


def cost(products, arrays):
    bytes_accessed = sum(math.prod(a.shape) * a.dtype.itemsize for a in arrays)
    return pl.CostEstimate(flops=6 * products, bytes_accessed=bytes_accessed, transcendentals=0)


def dot(a, b):
    return jnp.dot(a, b, preferred_element_type=F32)


def dot_nt(a, b):
    return lax.dot_general(a, b, (((1,), (1,)), ((), ())), preferred_element_type=F32)


def split(x):
    hi = x.astype(BF16)
    lo = (x - hi.astype(F32)).astype(BF16)
    return hi, lo


def dot_split(left_both, left_hi, right_hi, right_lo):
    both = dot(left_both, right_hi)
    rows = left_hi.shape[0]
    return both[:rows] + both[rows:] + dot(left_hi, right_lo)


def split_table(table):
    hi = table.astype(ml_dtypes.bfloat16)
    lo = (table - hi.astype(np.float64)).astype(ml_dtypes.bfloat16)
    return hi, lo


def primary(p, units):
    return units // 2 + 1 - p


def order(s, mirrored):
    i = 2 * s if s < ROWS // 2 else 2 * s - ROWS + 1
    return (ROWS - i) % ROWS if mirrored else i


def transform_tables(height, width):
    u_half, v_half = height // 2, width // 2
    pixels = height * width
    parity = np.arange(2)[:, None, None, None]
    u = 2 * np.arange(u_half)[:, None, None] + parity
    v = 2 * np.arange(v_half)[:, None, None] + parity
    h = np.arange(u_half)[:, None]
    w = np.arange(v_half)
    depth = u_half * v_half
    along_h = 2.0 * math.pi * np.broadcast_to(u * h / height, (2, u_half, u_half, v_half)).reshape(2, u_half, depth)
    along_w = 2.0 * math.pi * np.broadcast_to(v * w / width, (2, v_half, u_half, v_half)).reshape(2, v_half, depth)
    scale = 1.0 / math.sqrt(pixels)
    along_u = np.stack([np.cos(along_h), -np.sin(along_h)], axis=1) * scale
    along_v = np.stack([np.cos(along_w), -np.sin(along_w)], axis=1)
    factors = np.stack([along_u, along_v]).astype(np.float32)
    angle = along_h[:, None, :, None] + along_w[None, :, None, :]
    table = np.stack([np.cos(angle), -np.sin(angle)], axis=3) * scale
    forward, inverse = [], []
    for p in range(2):
        count = primary(p, u_half)
        rows = table[p, :, :count].reshape(2, count * 2 * v_half, depth)
        forward.append(np.concatenate(split_table(rows), axis=1))
        back = table[p, :, : u_half // 2].reshape(2, u_half // 2, 2, v_half // ROWS, ROWS, depth)
        back = np.transpose(back, (0, 5, 2, 3, 1, 4)).reshape(2, depth, -1)
        inverse.append(np.concatenate(split_table(back), axis=1))
    middle = np.transpose(table[0, :, u_half // 2, :, :, :v_half], (0, 3, 1, 2)).reshape(2, v_half, 2 * v_half)
    inverse.append(np.concatenate(split_table(middle), axis=1))
    return factors, forward, inverse


def low_rows(shape, rows):
    return lax.broadcasted_iota(jnp.int32, shape, len(shape) - 2) < rows


def roll_half(x):
    return pltpu.roll(x, ROWS // 2, x.ndim - 2)


def fold(quads, xs, p):
    left, right = (quads[0][b] + quads[1][b] if p == 0 else quads[0][b] - quads[1][b] for b in range(2))
    for q in range(2):
        xs[p, q, 0], xs[p, q, 1] = split(left + right if q == 0 else left - right)


def mirror(tiles, vb, low):
    return jnp.where(low, tiles[-vb % len(tiles)], tiles[len(tiles) - 1 - vb])


def forward_part(table_ref, xs, out_ref, p):
    units, _, blocks, _, _, _ = out_ref.shape
    channels = xs.shape[-1]
    groups = channels // LANES
    count = primary(p, units)
    both = []
    for q in range(2):
        table = table_ref[q]
        value = dot_split(table, table[: table.shape[0] // 2], xs[p, q, 0], xs[p, q, 1])
        both.append(value.reshape(count, 2, blocks // 2, ROWS, channels))
    low = low_rows((count, ROWS, LANES), ROWS // 2)
    first = low_rows((count, ROWS, LANES), 1)
    for piece in range(2):
        for group in range(groups):
            lanes = slice(group * LANES, (group + 1) * LANES)
            t = piece * groups + group
            tiles = []
            for k in range(blocks // 2):
                even, odd = (value[:, piece, k, :, lanes] for value in both)
                tiles.append(jnp.where(low, even, roll_half(odd)))
                tiles.append(jnp.where(low, roll_half(even), odd))
            for vb in range(blocks):
                out_ref[:count, p, vb, t] = tiles[vb]
                mirrored = mirror(tiles, vb, first)
                if piece == 1:
                    mirrored = -mirrored
                for unit in range(count, units):
                    out_ref[unit, p, vb, t] = mirrored[units - p - unit]


def join_parities(tiles):
    low = low_rows(tiles[0].shape, ROWS // 2)
    rows = tiles[0].shape[0] * ROWS
    evens, odds = [], []
    for k in range(len(tiles) // 2):
        one, two = tiles[2 * k], tiles[2 * k + 1]
        evens.append(jnp.where(low, one, roll_half(two)).reshape(rows, LANES))
        odds.append(jnp.where(low, roll_half(one), two).reshape(rows, LANES))
    return evens, odds


def gather_parity(m_ref, p, t):
    units, _, blocks, groups, _, _ = m_ref.shape
    half = units // 2
    first = low_rows((half, ROWS, LANES), 1)
    turned = []
    for vb in range(blocks):
        others = [m_ref[units - p - unit, p, vb, t] for unit in range(1 - p, half)]
        if p == 0:
            others.insert(0, jnp.zeros_like(others[0]))
        turned.append(jnp.stack(others))
    tiles = []
    for vb in range(blocks):
        own, other = m_ref[:half, p, vb, t], mirror(turned, vb, first)
        tiles.append(own + other if t < groups // 2 else own - other)
    return join_parities(tiles)


def gather_middle(m_ref, p, t):
    half = m_ref.shape[0] // 2
    return join_parities([m_ref[half : half + 1, p, vb, t] for vb in range(m_ref.shape[2])])


def operands(gather, m_ref, p):
    groups = m_ref.shape[3]
    columns = [[], []]
    for group in range(groups // 2):
        real = gather(m_ref, p, group)
        imag = gather(m_ref, p, groups // 2 + group)
        for q in range(2):
            columns[q].append(jnp.concatenate(real[q] + imag[q], axis=0))
    return [split(jnp.concatenate(columns[q], axis=1)) for q in range(2)]


def product(table, pair, part=0, parts=1):
    rows = table.shape[0] // 2
    count = rows // parts
    hi = table[part * count : (part + 1) * count]
    if parts == 1:
        return dot_split(table, hi, *pair)
    lo = table[rows + part * count : rows + (part + 1) * count]
    return dot_split(jnp.concatenate([hi, lo], axis=0), hi, *pair)


def inverse_quads(m_ref, table_refs, bias, parts=1):
    even_ref, odd_ref, middle_ref = table_refs
    pairs = operands(gather_parity, m_ref, 0) + operands(gather_parity, m_ref, 1)
    middle = [product(middle_ref[q], pair) for q, pair in enumerate(operands(gather_middle, m_ref, 0))]
    for part in range(parts):
        values = [product((even_ref, odd_ref)[i // 2][i % 2], pair, part, parts) for i, pair in enumerate(pairs)]
        for q, value in enumerate(middle):
            repeats = values[q].shape[0] // (2 * value.shape[0])
            values[q] += jnp.concatenate([value, -value] * repeats, axis=0)
        yield join_quads(values, bias)


def join_quads(values, bias):
    ee, eo, oe, oo = values
    along_w = [[ee + eo, ee - eo], [oe + oo, oe - oo]]
    quads = []
    for a in range(2):
        row = []
        for b in range(2):
            even, odd = along_w[0][b], along_w[1][b]
            row.append(jnp.maximum((even + odd if a == 0 else even - odd) + bias, 0.0))
        quads.append(row)
    return quads


def forward_kernel(x_hbm, factors_hbm, out_ref, x_ref, factors_ref, sems, factor_sem, even_ref, odd_ref, xs):
    fetch_factors = pltpu.make_async_copy(factors_hbm, factors_ref, factor_sem)

    def fetch_x(a):
        return pltpu.make_async_copy(x_hbm.at[a], x_ref.at[a], sems.at[a])

    fetch_factors.start()
    for a in range(2):
        fetch_x(a).start()
    fetch_factors.wait()
    units = factors_ref.shape[3]
    tables = (even_ref, odd_ref)
    for p in range(2):
        count = primary(p, units)
        for q in range(2):
            cos_v, sin_v = factors_ref[1, q, 0], factors_ref[1, q, 1]
            for u in range(count):
                cos_u = factors_ref[0, p, 0, u : u + 1, :]
                sin_u = factors_ref[0, p, 1, u : u + 1, :]
                real = cos_u * cos_v - sin_u * sin_v
                imag = sin_u * cos_v + cos_u * sin_v
                hi, lo = split(jnp.concatenate([real, imag], axis=0))
                rows = 2 * units
                tables[p][q, u * rows : (u + 1) * rows] = hi
                tables[p][q, (count + u) * rows : (count + u + 1) * rows] = lo
    for a in range(2):
        fetch_x(a).wait()
    _, h, _, w, channels = x_ref.shape
    for p in range(2):
        fold([[x_ref[a, :, b].reshape(h * w, channels) for b in range(2)] for a in range(2)], xs, p)
        forward_part(tables[p], xs, out_ref, p)


def forward(x, factors, tables):
    _, h, _, w, channels = x.shape
    out = jax.ShapeDtypeStruct((h, 2, 2 * w // ROWS, 2 * channels // LANES, ROWS, LANES), F32)
    return pl.pallas_call(
        forward_kernel,
        in_specs=[HBM, HBM],
        out_specs=VMEM,
        out_shape=out,
        scratch_shapes=[
            pltpu.VMEM(x.shape, F32),
            pltpu.VMEM(factors.shape, F32),
            pltpu.SemaphoreType.DMA((2,)),
            pltpu.SemaphoreType.DMA,
            *(pltpu.VMEM(t.shape, BF16) for t in tables),
            pltpu.VMEM((2, 2, 2, h * w, channels), BF16),
        ],
        compiler_params=pltpu.CompilerParams(vmem_limit_bytes=16 << 20),
        cost_estimate=cost(12 * sum(t.size for t in tables) // 2 * channels, (x, factors, out)),
        name="forward_transform",
    )(*(pltpu.with_memory_space_constraint(a, pltpu.HBM) for a in (x, factors)))


def inverse_kernel(layer, m_ref, even_ref, odd_ref, middle_ref, bias_ref, out_hbm, out_ref, sems):
    _, h, _, w, channels = out_ref.shape
    parts = sems.shape[0]
    rows = h // parts

    def write(part, a):
        at = pl.ds(part * rows, rows)
        return pltpu.make_async_copy(out_ref.at[a, at], out_hbm.at[a, at], sems.at[part, a])

    bias = bias_ref[layer : layer + 1, :]
    for part, quads in enumerate(inverse_quads(m_ref, (even_ref, odd_ref, middle_ref), bias, parts)):
        for a in range(2):
            for b in range(2):
                out_ref[a, part * rows : (part + 1) * rows, b] = quads[a][b].reshape(rows, w, channels)
            write(part, a).start()
    for part in range(parts):
        for a in range(2):
            write(part, a).wait()


def inverse(m, tables, bias, layer, shape):
    out = jax.ShapeDtypeStruct(shape, F32)
    return pl.pallas_call(
        functools.partial(inverse_kernel, layer),
        in_specs=[VMEM] * 5,
        out_specs=HBM,
        out_shape=out,
        scratch_shapes=[pltpu.VMEM(shape, F32), pltpu.SemaphoreType.DMA((2, 2))],
        compiler_params=pltpu.CompilerParams(vmem_limit_bytes=16 << 20),
        cost_estimate=cost(sum(t.size for t in tables) // 2 * shape[-1], (m, *tables, out)),
        name="inverse_transform",
    )(m, *tables, bias)


def turn_kernel(layer, m_ref, back_even, back_odd, back_middle, bias_ref, even_ref, odd_ref, out_ref, xs):
    tables = (back_even, back_odd, back_middle)
    (quads,) = inverse_quads(m_ref, tables, bias_ref[layer : layer + 1, :])
    for p, table_ref in enumerate((even_ref, odd_ref)):
        fold(quads, xs, p)
        forward_part(table_ref, xs, out_ref, p)


def turn(m, back_tables, bias, layer, tables):
    channels = bias.shape[1]
    return pl.pallas_call(
        functools.partial(turn_kernel, layer),
        in_specs=[VMEM] * 7,
        out_specs=VMEM,
        out_shape=jax.ShapeDtypeStruct(m.shape, F32),
        scratch_shapes=[pltpu.VMEM((2, 2, 2, tables[0].shape[-1], channels), BF16)],
        compiler_params=pltpu.CompilerParams(vmem_limit_bytes=16 << 20),
        cost_estimate=cost(sum(t.size for t in (*back_tables, *tables)) // 2 * channels, (m, *back_tables, *tables, m)),
        name="turn",
    )(m, *back_tables, bias, *tables)


def mix_kernel(layer, is_mirrored, v_ref, a_ref, out_ref, vs, ys):
    images, groups, per, _ = v_ref.shape
    for t in range(groups):
        hi, lo = split(jnp.transpose(v_ref[:, t], (1, 0, 2)))
        lanes = slice(t * LANES, (t + 1) * LANES)
        vs[:, :images, lanes] = hi
        vs[:, images:, lanes] = lo
    mirrored = is_mirrored()
    for s in range(per):
        i = jnp.where(mirrored, order(s, True), order(s, False))
        a_hi, a_lo = split(a_ref[layer, i])
        both = dot_nt(vs[s], a_hi)
        low_part = dot_nt(a_lo, vs[s, :images])
        for t in range(groups):
            lanes = slice(t * LANES, (t + 1) * LANES)
            ys[t, s] = both[:images, lanes] + both[images:, lanes] + low_part[lanes].T
    for t in range(groups):
        out_ref[:, t] = jnp.transpose(ys[t], (1, 0, 2))


def mix(v, blocks, layer, is_mirrored):
    images, groups, per, _ = v.shape
    both = blocks.shape[-1]
    return pl.pallas_call(
        functools.partial(mix_kernel, layer, is_mirrored),
        in_specs=[VMEM, VMEM],
        out_specs=VMEM,
        out_shape=jax.ShapeDtypeStruct(v.shape, F32),
        scratch_shapes=[
            pltpu.VMEM((per, 2 * images, both), BF16),
            pltpu.VMEM((groups, per, images, LANES), F32),
        ],
        compiler_params=pltpu.CompilerParams(vmem_limit_bytes=16 << 20),
        cost_estimate=cost(v.size * both, (v, v, blocks)),
        name="mix",
    )(v, blocks)


def body(images, blocks, bias):
    _, channels, height, width = images.shape
    pixels = height * width
    factors, tables, back_tables = jax.tree.map(jnp.asarray, transform_tables(height, width))

    def exchange(value):
        return lax.all_to_all(value, ("gx", "gy"), split_axis=0, concat_axis=0, tiled=True)

    sent = (lax.axis_size(("gx", "gy")), 2 * channels // LANES, ROWS, LANES)
    quads = (2, height // 2, 2, width // 2, channels)

    def is_mirrored():
        u = (lax.axis_index("gx") * lax.axis_size("gy") + lax.axis_index("gy")) // (width // ROWS)
        return u > height // 2

    def mixed(v, layer):
        held = exchange(v.reshape(sent))
        return exchange(mix(held, blocks, layer, is_mirrored)).reshape(v.shape)

    x = images.reshape(channels, pixels).T.reshape(quads)
    m = mixed(forward(x, factors, tables), 0)
    m = mixed(turn(m, back_tables, bias, 0, tables), 1)
    out = inverse(m, back_tables, bias, 1, quads)
    return out.reshape(pixels, channels).T.reshape(1, channels, height, width)


def solution(mesh):
    placed = (P(("gx", "gy"), None, None, None), P(None, ("gx", "gy"), None, None), P())
    return jax.shard_map(
        body,
        mesh=mesh,
        in_specs=placed,
        out_specs=P(("gx", "gy"), None, None, None),
        check_vma=False,
    )
```
